32 devices in a mesh: chan: 8 (over y, x, core), space: 4 (over z).
Axes of the slice: x: 2, y: 2, z: 4, core: 2. Of those that a mesh axis runs over, the one named last changes fastest.
Arguments:
- u_rows: int32 [64, 8192], P('chan', 'space'), may hold values from 0 to 8191, as said below
- v_cols: int32 [64, 8192], P('chan', 'space'), may hold values from 0 to 8191
- weights: float32 [64, 8192], P('chan', 'space'), may hold values from 0.1 to 10
- tau: float32 [64], P('chan'), may hold values from -0.75 to 0.75
- crop_start: int32 [2], replicated, may hold values from 0 to 8064
Outputs:
- psf: float32 [5, 128, 128], replicated
The draws below stay inside these ranges and needn't reach their ends.
Inputs may be any that keep to these rules, and one draw needn't show every extreme that they name: u_rows[c, j] lies in row tile j // 2048: from (j // 2048) * 2048 to (j // 2048 + 1) * 2048 - 1.
All inputs are finite; a program needn't handle non-finite values.
Results may differ from the reference program's by a relative error of at most 0.0032.
Values sent between devices are 32-bit elements; how exact they have to be, the bound alone decides.
No kernel may reach another device: no remote copies, remote signals or barrier semaphores. Data moves between devices by JAX's collectives and lax.ppermute only.
A program may use at most 128 MiB of HBM per device.

```python
import math
import jax
import jax.numpy as jnp
from jax import lax

G = 8192
P_SIZE = 128
TERMS = 5
CH_DEV = 8
NV = 2048
NCHAN = 64
NVIS = 8192
N_CHAN = 8
N_SPACE = 4


def draw_u_rows(key, part):
    tile_ids = jnp.arange(N_SPACE * NV, dtype=jnp.int32) // NV
    offsets = jax.random.randint(key, (CH_DEV * N_CHAN, N_SPACE * NV), 0, G // N_SPACE, dtype=jnp.int32)
    return offsets + tile_ids[None, :] * (G // N_SPACE)


def set_ends(entries, rng, least, largest):
    longest = entries.shape.index(max(entries.shape))
    spots = []
    for shift in (0, 1):
        where = [jax.random.randint(jax.random.fold_in(rng, axis), (), 0, length) for axis, length in enumerate(entries.shape)]
        where[longest] = (where[longest] + shift) % entries.shape[longest]
        spots.append(tuple(where))
    return entries.at[spots[0]].set(least).at[spots[1]].set(largest)


def block_levels(rng, shape, pieces, low, high):
    def one(dim, blocks):
        heights = jax.random.uniform(jax.random.fold_in(jax.random.fold_in(rng, 6), dim), (blocks,), jnp.float32, low / len(pieces), high / len(pieces))
        return jnp.repeat(jnp.exp(heights), shape[dim] // blocks).reshape((-1,) + (1,) * (len(shape) - dim - 1))

    loudness = one(*pieces[0])
    for cut in pieces[1:]:
        loudness = loudness * one(*cut)
    return loudness


def setup_inputs(seed: int = 0) -> dict:
    key_list = jax.random.split(jax.random.key(seed), 6)
    u_rows = draw_u_rows(jax.random.fold_in(key_list[5], 71), 0)
    v_cols = set_ends(jax.random.randint(key_list[1], (NCHAN, NVIS), 0, G), jax.random.fold_in(key_list[1], 1), 0, G - 1).astype(jnp.int32)
    weights = jnp.clip(jnp.exp(math.log(10.0) - 4.6051702 * jax.random.uniform(key_list[2], (NCHAN, NVIS), jnp.float32) ** block_levels(key_list[2], (NCHAN, NVIS), ((0, 8), (1, 4)), -0.2, 0.2)), 0.1, 10.0)
    tau = jnp.clip(jax.random.uniform(key_list[3], (NCHAN,), jnp.float32, -0.75, 0.75) * block_levels(key_list[3], (NCHAN,), ((0, 8),), -0.4, 0.0), -0.75, 0.75)
    crop_start = jax.random.randint(key_list[4], (2,), 0, G - P_SIZE + 1).astype(jnp.int32)
    return {"u_rows": u_rows, "v_cols": v_cols, "weights": weights, "tau": tau, "crop_start": crop_start}


def col_tables(columns_in, weight_row, crop_start):
    columns = crop_start[1] + jnp.arange(P_SIZE, dtype=jnp.int32)
    phases = columns_in[..., None] * columns % G
    angles = phases.astype(jnp.float32) * (2.0 * math.pi / G)
    scaled = weight_row[..., None]
    return jnp.concatenate([scaled * jnp.cos(angles), scaled * jnp.sin(angles)], axis=-1).astype(jnp.bfloat16)

def taylor_powers(tau):
    terms_list = [jnp.ones_like(tau)]
    for degree in range(TERMS - 1):
        terms_list.append(terms_list[-1] * tau)
    return jnp.stack(terms_list, axis=-1)

def row_transform(row_ids, grids, crop_start):
    lines = crop_start[0] + jnp.arange(P_SIZE, dtype=jnp.int32)
    phases = lines[:, None] * row_ids[None, :] % G
    angles = phases.astype(jnp.float32) * (2.0 * math.pi / G)
    flat = grids.reshape(grids.shape[0], TERMS * 2 * P_SIZE)
    cos_part = jnp.dot(jnp.cos(angles), flat, precision=lax.Precision.HIGHEST, preferred_element_type=jnp.float32).reshape(P_SIZE, TERMS, 2 * P_SIZE)
    sin_part = jnp.dot(jnp.sin(angles), flat, precision=lax.Precision.HIGHEST, preferred_element_type=jnp.float32).reshape(P_SIZE, TERMS, 2 * P_SIZE)
    return jnp.transpose(cos_part[:, :, :P_SIZE] - sin_part[:, :, P_SIZE:], (1, 0, 2))

def reference(u_rows, v_cols, weights, tau, crop_start):
    powers = taylor_powers(tau)

    def add_channel(carry, inputs):
        rows_in, cols_in, weight_row, power = inputs
        tables = col_tables(cols_in, weight_row, crop_start).astype(jnp.float32)
        grids = jnp.zeros((G, 2 * P_SIZE), jnp.float32).at[rows_in].add(tables)
        return (carry + power[None, :, None] * grids[:, None, :], None)
    taylor, _ = lax.scan(add_channel, jnp.zeros((G, TERMS, 2 * P_SIZE), jnp.float32), (u_rows, v_cols, weights, powers))
    beam_sum = row_transform(jnp.arange(G, dtype=jnp.int32), taylor, crop_start)
    return beam_sum / jnp.sqrt(jnp.sum(weights * weights))
```

```python
import functools
import math

import jax
import jax.numpy as jnp
from jax import lax
from jax.experimental import pallas as pl
from jax.experimental.pallas import tpu as pltpu
from jax.sharding import PartitionSpec as P

G = 8192
P_SIZE = 128
TERMS = 5
HALF = P_SIZE // 2
STEP = 8
WIDTH = 256
QUARTER = G // 4


def sin_cos(phase):
    quadrant = (phase + QUARTER // 2) >> (QUARTER.bit_length() - 1)
    rest = phase - quadrant * QUARTER
    x = rest.astype(jnp.float32) * (2.0 * math.pi / G)
    z = x * x
    s = x + x * z * (-1.6666654611e-1 + z * (8.3321608736e-3 + z * -1.9515295891e-4))
    c = 1.0 - 0.5 * z + z * z * (4.166664568298827e-2 + z * (-1.388731625493765e-3 + z * 2.443315711809948e-5))
    odd = (quadrant & 1) == 1
    sin_value = jnp.where(odd, c, s)
    cos_value = jnp.where(odd, s, c)
    sin_value = jnp.where((quadrant & 2) == 2, -sin_value, sin_value)
    cos_value = jnp.where(((quadrant + 1) & 2) == 2, -cos_value, cos_value)
    return cos_value, sin_value


def fill_table(table, chunk, ids, start, cos_step, sin_step, scale):
    width = ids.shape[1]
    row = lax.broadcasted_iota(jnp.int32, (STEP, width), 0)
    ids = jnp.broadcast_to(ids, (STEP, width))
    cos_prev, sin_prev = sin_cos((ids * (row + start)) & (G - 1))
    if scale is not None:
        scale = jnp.broadcast_to(scale, (STEP, width))
        cos_prev, sin_prev = cos_prev * scale, sin_prev * scale
    cos_step = jnp.broadcast_to(cos_step, (STEP, width))
    sin_step = jnp.broadcast_to(sin_step, (STEP, width))
    cos_now = cos_prev * cos_step - sin_prev * sin_step
    sin_now = sin_prev * cos_step + cos_prev * sin_step
    twice = cos_step + cos_step
    for first in range(0, P_SIZE, 2 * STEP):
        table[first : first + 2 * STEP, chunk] = jnp.concatenate([cos_prev, cos_now], axis=0).astype(jnp.bfloat16)
        table[P_SIZE + first : P_SIZE + first + 2 * STEP, chunk] = jnp.concatenate(
            [sin_prev, sin_now], axis=0
        ).astype(jnp.bfloat16)
        if first + 2 * STEP < P_SIZE:
            cos_prev = twice * cos_now - cos_prev
            sin_prev = twice * sin_now - sin_prev
            cos_now = twice * cos_prev - cos_now
            sin_now = twice * sin_prev - sin_now


def kernel(
    place_ref, tau_ref, u_ref, v_ref, w_ref, mine_ref, other_ref, row_tables, col_tables, steps, beams
):
    channels, count = u_ref.shape
    row_start, col_start, core = place_ref[0], place_ref[1], place_ref[2]
    for k, ref in enumerate((u_ref, v_ref)):
        cos_step, sin_step = sin_cos((ref[...] * STEP) & (G - 1))
        steps[2 * k], steps[2 * k + 1] = cos_step, sin_step
    beams[...] = jnp.zeros_like(beams)

    def fill(channel, slot):
        one = slice(channel, channel + 1)
        for begin in range(0, count, WIDTH):
            chunk = slice(begin, begin + WIDTH)
            fill_table(
                row_tables.at[slot], chunk, u_ref[one, chunk], row_start, steps[0, one, chunk], steps[1, one, chunk], None
            )
            fill_table(
                col_tables.at[slot],
                chunk,
                v_ref[one, chunk],
                col_start,
                steps[2, one, chunk],
                steps[3, one, chunk],
                w_ref[one, chunk],
            )

    def add(channel, slot):
        product = lax.dot_general(
            row_tables[slot], col_tables[slot], (((1,), (1,)), ((), ())), preferred_element_type=jnp.float32
        )
        beam = product[:P_SIZE, :P_SIZE] - product[P_SIZE:, P_SIZE:]
        tau = tau_ref[channel]
        power = jnp.float32(1.0)
        for term in range(TERMS):
            beams[term] += power * beam
            power = power * tau

    fill(0, 0)
    for channel in range(channels):
        if channel + 1 < channels:
            fill(channel + 1, (channel + 1) % 2)
        add(channel, channel % 2)

    squares = jnp.zeros((channels, P_SIZE), jnp.float32)
    for begin in range(0, count, P_SIZE):
        w = w_ref[:, begin : begin + P_SIZE]
        squares += w * w

    def put(low, high):
        for ref, first in ((low, 0), (high, HALF)):
            for term in range(TERMS):
                ref[term * HALF : (term + 1) * HALF, :] = beams[term, first : first + HALF, :]
            ref[TERMS * HALF :, :] = squares

    pl.when(core == 0)(lambda: put(mine_ref, other_ref))
    pl.when(core == 1)(lambda: put(other_ref, mine_ref))


def partial_beams(u_rows, v_cols, weights, tau, place):
    channels, count = u_rows.shape
    rows = TERMS * HALF + channels
    part = jax.ShapeDtypeStruct((rows, P_SIZE), jnp.float32)
    vmem = pl.BlockSpec(memory_space=pltpu.VMEM)
    smem = pl.BlockSpec(memory_space=pltpu.SMEM)
    return pl.pallas_call(
        kernel,
        out_shape=(part, part),
        in_specs=[smem, smem, vmem, vmem, vmem],
        out_specs=(vmem, vmem),
        scratch_shapes=[
            pltpu.VMEM((2, 2 * P_SIZE, count), jnp.bfloat16),
            pltpu.VMEM((2, 2 * P_SIZE, count), jnp.bfloat16),
            pltpu.VMEM((4, channels, count), jnp.float32),
            pltpu.VMEM((TERMS, P_SIZE, P_SIZE), jnp.float32),
        ],
    )(place, tau, u_rows, v_cols, weights)


def exchange_orders(chan, space):
    over_chan = [("chan", 1 << b) for b in range(1, chan.bit_length() - 1)]
    over_space = [("space", 1 << b) for b in range(space.bit_length() - 1)]
    first = []
    for k in range(max(len(over_chan), len(over_space))):
        first += over_chan[k : k + 1] + over_space[k : k + 1]
    second = list(first)
    for k in range(0, len(second) - 1, 2):
        second[k], second[k + 1] = second[k + 1], second[k]
    return first, second


def on_device(u_rows, v_cols, weights, tau, crop_start):
    chan, space = lax.axis_size("chan"), lax.axis_size("space")
    core = lax.axis_index("chan") % 2
    place = jnp.concatenate([crop_start, core[None]])
    mine, other = partial_beams(u_rows, v_cols, weights, tau, place)
    partner = [(i, i ^ 1) for i in range(chan)]
    total = mine + lax.ppermute(other, "chan", partner)
    for moves in zip(*exchange_orders(chan, space)):
        pairs = []
        for c in range(chan):
            axis, bit = moves[c % 2]
            for s in range(space):
                to = (c ^ bit, s) if axis == "chan" else (c, s ^ bit)
                pairs.append((c * space + s, to[0] * space + to[1]))
        total = total + lax.ppermute(total, ("chan", "space"), pairs)
    beam = total[: TERMS * HALF] / jnp.sqrt(jnp.sum(total[TERMS * HALF :]))
    away = lax.ppermute(beam, "chan", partner)
    low = jnp.where(core == 0, beam, away).reshape(TERMS, HALF, P_SIZE)
    high = jnp.where(core == 0, away, beam).reshape(TERMS, HALF, P_SIZE)
    return jnp.concatenate([low, high], axis=1)


def solution(mesh):
    in_specs = (P("chan", "space"), P("chan", "space"), P("chan", "space"), P("chan"), P())
    return jax.shard_map(on_device, mesh=mesh, in_specs=in_specs, out_specs=P(), check_vma=False)
```

```python
import math

import jax
import jax.numpy as jnp
from jax import lax
from jax.experimental import pallas as pl
from jax.experimental.pallas import tpu as pltpu
from jax.sharding import PartitionSpec as P

G = 8192
P_SIZE = 128
TERMS = 5
HALF = P_SIZE // 2
STEP = 8
WIDTH = 128
QUARTER = G // 4


def sin_cos(phase):
    quadrant = (phase + QUARTER // 2) >> (QUARTER.bit_length() - 1)
    rest = phase - quadrant * QUARTER
    x = rest.astype(jnp.float32) * (2.0 * math.pi / G)
    z = x * x
    s = x + x * z * (-1.6666654611e-1 + z * (8.3321608736e-3 + z * -1.9515295891e-4))
    c = 1.0 - 0.5 * z + z * z * (4.166664568298827e-2 + z * (-1.388731625493765e-3 + z * 2.443315711809948e-5))
    odd = (quadrant & 1) == 1
    sin_value = jnp.where(odd, c, s)
    cos_value = jnp.where(odd, s, c)
    sin_value = jnp.where((quadrant & 2) == 2, -sin_value, sin_value)
    cos_value = jnp.where(((quadrant + 1) & 2) == 2, -cos_value, cos_value)
    return cos_value, sin_value


def prepare(ids, start, scale, seeds, steps):
    cos_one, sin_one = sin_cos(ids)
    cos_prev, sin_prev = sin_cos((ids * start) & (G - 1))
    if scale is not None:
        cos_prev, sin_prev = cos_prev * scale, sin_prev * scale
    cos_now = cos_prev * cos_one - sin_prev * sin_one
    sin_now = sin_prev * cos_one + cos_prev * sin_one
    twice = cos_one + cos_one
    channels, count = ids.shape
    for row in range(STEP):
        rows = pl.ds(row, channels, stride=STEP)
        for group in range(count // WIDTH):
            chunk = slice(group * WIDTH, (group + 1) * WIDTH)
            seeds[0, group, rows, :] = cos_prev[:, chunk]
            seeds[1, group, rows, :] = sin_prev[:, chunk]
        cos_prev, cos_now = cos_now, twice * cos_now - cos_prev
        sin_prev, sin_now = sin_now, twice * sin_now - sin_prev
    steps[0], steps[1] = sin_cos((ids * STEP) & (G - 1))


def fill_table(table, chunk, cos_prev, sin_prev, cos_step, sin_step):
    cos_step = jnp.broadcast_to(cos_step, cos_prev.shape)
    sin_step = jnp.broadcast_to(sin_step, cos_prev.shape)
    cos_now = cos_prev * cos_step - sin_prev * sin_step
    sin_now = sin_prev * cos_step + cos_prev * sin_step
    twice = cos_step + cos_step
    for first in range(0, P_SIZE, 2 * STEP):
        table[first : first + 2 * STEP, chunk] = jnp.concatenate([cos_prev, cos_now], axis=0).astype(jnp.bfloat16)
        table[P_SIZE + first : P_SIZE + first + 2 * STEP, chunk] = jnp.concatenate(
            [sin_prev, sin_now], axis=0
        ).astype(jnp.bfloat16)
        if first + 2 * STEP < P_SIZE:
            cos_prev = twice * cos_now - cos_prev
            sin_prev = twice * sin_now - sin_prev
            cos_now = twice * cos_prev - cos_now
            sin_now = twice * sin_prev - sin_now


def half_of(chan, space):
    bits = chan ^ space
    for shift in (16, 8, 4, 2, 1):
        bits = bits ^ (bits >> shift)
    return bits & 1


def kernel(
    crop_hbm,
    tau_hbm,
    u_hbm,
    v_hbm,
    w_hbm,
    mine_ref,
    other_ref,
    crop_ref,
    tau_ref,
    u_ref,
    v_ref,
    w_ref,
    row_tables,
    col_tables,
    seeds,
    steps,
    beams,
    arrived,
):
    channels, count = u_ref.shape
    copies = [
        pltpu.make_async_copy(source, target, arrived.at[k])
        for k, (source, target) in enumerate(
            ((crop_hbm, crop_ref), (u_hbm, u_ref), (v_hbm, v_ref), (w_hbm, w_ref), (tau_hbm, tau_ref))
        )
    ]
    for copy in copies:
        copy.start()
    for copy in copies[:2]:
        copy.wait()
    prepare(u_ref[...], crop_ref[0], None, seeds.at[0], steps.at[0])
    for copy in copies[2:]:
        copy.wait()
    prepare(v_ref[...], crop_ref[1], w_ref[...], seeds.at[1], steps.at[1])
    beams[...] = jnp.zeros_like(beams)

    def fill(channel, slot):
        one = slice(channel, channel + 1)
        rows = slice(channel * STEP, (channel + 1) * STEP)
        for group in range(0, count // WIDTH, 2):
            chunk = slice(group * WIDTH, (group + 2) * WIDTH)
            for side, tables in enumerate((row_tables, col_tables)):
                seed = [
                    jnp.concatenate([seeds[side, k, group, rows, :], seeds[side, k, group + 1, rows, :]], axis=1)
                    for k in range(2)
                ]
                fill_table(
                    tables.at[slot],
                    chunk,
                    *seed,
                    steps[side, 0, one, chunk],
                    steps[side, 1, one, chunk],
                )

    def add(channel, slot):
        product = lax.dot_general(
            row_tables[slot], col_tables[slot], (((1,), (1,)), ((), ())), preferred_element_type=jnp.float32
        )
        beam = product[:P_SIZE, :P_SIZE] - product[P_SIZE:, P_SIZE:]
        tau = tau_ref[channel]
        power = jnp.float32(1.0)
        for term in range(TERMS):
            beams[term] += power * beam
            power = power * tau

    fill(0, 0)
    for channel in range(channels):
        if channel + 1 < channels:
            fill(channel + 1, (channel + 1) % 2)
        add(channel, channel % 2)

    squares = jnp.zeros((channels, P_SIZE), jnp.float32)
    for begin in range(0, count, P_SIZE):
        w = w_ref[:, begin : begin + P_SIZE]
        squares += w * w

    def put(low, high):
        for ref, first in ((low, 0), (high, HALF)):
            for term in range(TERMS):
                ref[term * HALF : (term + 1) * HALF, :] = beams[term, first : first + HALF, :]
            ref[TERMS * HALF :, :] = squares

    half = half_of(lax.axis_index("chan"), lax.axis_index("space"))
    pl.when(half == 0)(lambda: put(mine_ref, other_ref))
    pl.when(half == 1)(lambda: put(other_ref, mine_ref))


def finish(mine_ref, away_ref, psf_ref):
    squares = mine_ref[TERMS * HALF :, :]
    scale = 1.0 / jnp.sqrt(jnp.sum(jnp.sum(squares, axis=1, keepdims=True), axis=0, keepdims=True))

    def put(low, high):
        for ref, first in ((low, 0), (high, HALF)):
            for term in range(TERMS):
                psf_ref[term, first : first + HALF, :] = ref[term * HALF : (term + 1) * HALF, :] * scale

    half = half_of(lax.axis_index("chan"), lax.axis_index("space"))
    pl.when(half == 0)(lambda: put(mine_ref, away_ref))
    pl.when(half == 1)(lambda: put(away_ref, mine_ref))


VMEM = pl.BlockSpec(memory_space=pltpu.VMEM)
HBM = pl.BlockSpec(memory_space=pltpu.HBM)


def partial_beams(u_rows, v_cols, weights, tau, crop_start):
    channels, count = u_rows.shape
    rows = TERMS * HALF + channels
    part = jax.ShapeDtypeStruct((rows, P_SIZE), jnp.float32)
    return pl.pallas_call(
        kernel,
        out_shape=(part, part),
        in_specs=[HBM] * 5,
        out_specs=(VMEM, VMEM),
        scratch_shapes=[
            pltpu.SMEM(crop_start.shape, crop_start.dtype),
            pltpu.SMEM(tau.shape, tau.dtype),
            pltpu.VMEM(u_rows.shape, u_rows.dtype),
            pltpu.VMEM(v_cols.shape, v_cols.dtype),
            pltpu.VMEM(weights.shape, weights.dtype),
            pltpu.VMEM((2, 2 * P_SIZE, count), jnp.bfloat16),
            pltpu.VMEM((2, 2 * P_SIZE, count), jnp.bfloat16),
            pltpu.VMEM((2, 2, count // WIDTH, channels * STEP, WIDTH), jnp.float32),
            pltpu.VMEM((2, 2, channels, count), jnp.float32),
            pltpu.VMEM((TERMS, P_SIZE, P_SIZE), jnp.float32),
            pltpu.SemaphoreType.DMA((5,)),
        ],
        compiler_params=pltpu.CompilerParams(vmem_limit_bytes=16 << 20),
    )(*(pltpu.with_memory_space_constraint(x, pltpu.HBM) for x in (crop_start, tau, u_rows, v_cols, weights)))


def whole_patch(mine, away):
    return pl.pallas_call(
        finish,
        out_shape=jax.ShapeDtypeStruct((TERMS, P_SIZE, P_SIZE), jnp.float32),
        in_specs=[VMEM, VMEM],
        out_specs=VMEM,
        compiler_params=pltpu.CompilerParams(vmem_limit_bytes=4 << 20),
    )(mine, away)


def exchange_orders(chan, space):
    over_chan = [("chan", 1 << b) for b in range(1, chan.bit_length() - 1)]
    over_space = [("space", 1 << b) for b in range(space.bit_length() - 1)]
    first = []
    for k in range(max(len(over_chan), len(over_space))):
        first += over_chan[k : k + 1] + over_space[k : k + 1]
    second = list(first)
    for k in range(0, len(second) - 1, 2):
        second[k], second[k + 1] = second[k + 1], second[k]
    return first, second


def pairs_of(moves, chan, space):
    pairs = []
    for c in range(chan):
        for s in range(space):
            axis, bit = moves[half_of(c, s)]
            to = (c ^ bit ^ 1, s) if axis == "chan" else (c ^ 1, s ^ bit)
            pairs.append((c * space + s, to[0] * space + to[1]))
    return pairs


def on_device(u_rows, v_cols, weights, tau, crop_start):
    chan, space = lax.axis_size("chan"), lax.axis_size("space")
    mine, other = partial_beams(u_rows, v_cols, weights, tau, crop_start)
    partner = [(i, i ^ 1) for i in range(chan)]
    total = mine + lax.ppermute(other, "chan", partner)
    for moves in zip(*exchange_orders(chan, space)):
        total = total + lax.ppermute(total, ("chan", "space"), pairs_of(moves, chan, space))
    return whole_patch(total, lax.ppermute(total, "chan", partner))


def solution(mesh):
    in_specs = (P("chan", "space"), P("chan", "space"), P("chan", "space"), P("chan"), P())
    return jax.shard_map(on_device, mesh=mesh, in_specs=in_specs, out_specs=P(), check_vma=False)
```

```python
import math

import jax
import jax.numpy as jnp
from jax import lax
from jax.experimental import pallas as pl
from jax.experimental.pallas import tpu as pltpu
from jax.sharding import PartitionSpec as P

G = 8192
P_SIZE = 128
TERMS = 5
STREAMS = 2
ROWS = P_SIZE // STREAMS
HALF = ROWS // 2
STEP = 8
WIDTH = 128
QUARTER = G // 4


def sin_cos(phase):
    quadrant = (phase + QUARTER // 2) >> (QUARTER.bit_length() - 1)
    rest = phase - quadrant * QUARTER
    x = rest.astype(jnp.float32) * (2.0 * math.pi / G)
    z = x * x
    s = x + x * z * (-1.6666654611e-1 + z * (8.3321608736e-3 + z * -1.9515295891e-4))
    c = 1.0 - 0.5 * z + z * z * (4.166664568298827e-2 + z * (-1.388731625493765e-3 + z * 2.443315711809948e-5))
    odd = (quadrant & 1) == 1
    sin_value = jnp.where(odd, c, s)
    cos_value = jnp.where(odd, s, c)
    sin_value = jnp.where((quadrant & 2) == 2, -sin_value, sin_value)
    cos_value = jnp.where(((quadrant + 1) & 2) == 2, -cos_value, cos_value)
    return cos_value, sin_value


def prepare(ids, start, scale, seeds, steps):
    cos_one, sin_one = sin_cos(ids)
    cos_prev, sin_prev = sin_cos((ids * start) & (G - 1))
    if scale is not None:
        cos_prev, sin_prev = cos_prev * scale, sin_prev * scale
    cos_now = cos_prev * cos_one - sin_prev * sin_one
    sin_now = sin_prev * cos_one + cos_prev * sin_one
    twice = cos_one + cos_one
    channels, count = ids.shape
    for row in range(STEP):
        rows = pl.ds(row, channels, stride=STEP)
        for group in range(count // WIDTH):
            chunk = slice(group * WIDTH, (group + 1) * WIDTH)
            seeds[0, group, rows, :] = cos_prev[:, chunk]
            seeds[1, group, rows, :] = sin_prev[:, chunk]
        cos_prev, cos_now = cos_now, twice * cos_now - cos_prev
        sin_prev, sin_now = sin_now, twice * sin_now - sin_prev
    steps[0], steps[1] = sin_cos((ids * STEP) & (G - 1))


def fill_table(table, chunk, cos_prev, sin_prev, cos_step, sin_step):
    cos_step = jnp.broadcast_to(cos_step, cos_prev.shape)
    sin_step = jnp.broadcast_to(sin_step, cos_prev.shape)
    cos_now = cos_prev * cos_step - sin_prev * sin_step
    sin_now = sin_prev * cos_step + cos_prev * sin_step
    twice = cos_step + cos_step
    for first in range(0, P_SIZE, 2 * STEP):
        table[first : first + 2 * STEP, chunk] = jnp.concatenate([cos_prev, cos_now], axis=0).astype(jnp.bfloat16)
        table[P_SIZE + first : P_SIZE + first + 2 * STEP, chunk] = jnp.concatenate(
            [sin_prev, sin_now], axis=0
        ).astype(jnp.bfloat16)
        if first + 2 * STEP < P_SIZE:
            cos_prev = twice * cos_now - cos_prev
            sin_prev = twice * sin_now - sin_prev
            cos_now = twice * cos_prev - cos_now
            sin_now = twice * sin_prev - sin_now


def half_of(chan, space):
    bits = chan ^ space
    for shift in (16, 8, 4, 2, 1):
        bits = bits ^ (bits >> shift)
    return bits & 1


def kernel(
    crop_hbm,
    tau_hbm,
    u_hbm,
    v_hbm,
    w_hbm,
    mine_a,
    other_a,
    mine_b,
    other_b,
    crop_ref,
    tau_ref,
    u_ref,
    v_ref,
    w_ref,
    row_tables,
    col_tables,
    seeds,
    steps,
    beams,
    arrived,
):
    channels, count = u_ref.shape
    copies = [
        pltpu.make_async_copy(source, target, arrived.at[k])
        for k, (source, target) in enumerate(
            ((crop_hbm, crop_ref), (u_hbm, u_ref), (v_hbm, v_ref), (w_hbm, w_ref), (tau_hbm, tau_ref))
        )
    ]
    for copy in copies:
        copy.start()
    for copy in copies[:2]:
        copy.wait()
    prepare(u_ref[...], crop_ref[0], None, seeds.at[0], steps.at[0])
    for copy in copies[2:]:
        copy.wait()
    prepare(v_ref[...], crop_ref[1], w_ref[...], seeds.at[1], steps.at[1])
    beams[...] = jnp.zeros_like(beams)

    def fill(channel, slot):
        one = slice(channel, channel + 1)
        rows = slice(channel * STEP, (channel + 1) * STEP)
        for group in range(0, count // WIDTH, 2):
            chunk = slice(group * WIDTH, (group + 2) * WIDTH)
            for side, tables in enumerate((row_tables, col_tables)):
                seed = [
                    jnp.concatenate([seeds[side, k, group, rows, :], seeds[side, k, group + 1, rows, :]], axis=1)
                    for k in range(2)
                ]
                fill_table(
                    tables.at[slot],
                    chunk,
                    *seed,
                    steps[side, 0, one, chunk],
                    steps[side, 1, one, chunk],
                )

    def add(channel, slot):
        product = lax.dot_general(
            row_tables[slot], col_tables[slot], (((1,), (1,)), ((), ())), preferred_element_type=jnp.float32
        )
        beam = product[:P_SIZE, :P_SIZE] - product[P_SIZE:, P_SIZE:]
        tau = tau_ref[channel]
        power = jnp.float32(1.0)
        for term in range(TERMS):
            beams[term] += power * beam
            power = power * tau

    fill(0, 0)
    for channel in range(channels):
        if channel + 1 < channels:
            fill(channel + 1, (channel + 1) % 2)
        add(channel, channel % 2)

    squares = jnp.zeros((channels, P_SIZE), jnp.float32)
    for begin in range(0, count, P_SIZE):
        w = w_ref[:, begin : begin + P_SIZE]
        squares += w * w

    mine_a[TERMS * HALF :, :] = squares
    other_a[TERMS * HALF :, :] = squares

    def put(half):
        for k, ref in enumerate((mine_a, other_a, mine_b, other_b)):
            first = first_row(k, half)
            for term in range(TERMS):
                ref[term * HALF : (term + 1) * HALF, :] = beams[term, first : first + HALF, :]

    half = half_of(lax.axis_index("chan"), lax.axis_index("space"))
    pl.when(half == 0)(lambda: put(0))
    pl.when(half == 1)(lambda: put(1))


def first_row(k, half):
    return (k // 2) * ROWS + (half ^ (k % 2)) * HALF


def finish(*refs):
    *parts, psf_ref = refs
    squares = parts[0][TERMS * HALF :, :]
    scale = 1.0 / jnp.sqrt(jnp.sum(jnp.sum(squares, axis=1, keepdims=True), axis=0, keepdims=True))

    def put(half):
        for k, ref in enumerate(parts):
            first = first_row(k, half)
            for term in range(TERMS):
                psf_ref[term, first : first + HALF, :] = ref[term * HALF : (term + 1) * HALF, :] * scale

    half = half_of(lax.axis_index("chan"), lax.axis_index("space"))
    pl.when(half == 0)(lambda: put(0))
    pl.when(half == 1)(lambda: put(1))


VMEM = pl.BlockSpec(memory_space=pltpu.VMEM)
HBM = pl.BlockSpec(memory_space=pltpu.HBM)


def partial_beams(u_rows, v_cols, weights, tau, crop_start):
    channels, count = u_rows.shape
    part_a, part_b = (jax.ShapeDtypeStruct((TERMS * HALF + extra, P_SIZE), jnp.float32) for extra in (channels, 0))
    return pl.pallas_call(
        kernel,
        out_shape=(part_a, part_a, part_b, part_b),
        in_specs=[HBM] * 5,
        out_specs=(VMEM,) * 4,
        scratch_shapes=[
            pltpu.SMEM(crop_start.shape, crop_start.dtype),
            pltpu.SMEM(tau.shape, tau.dtype),
            pltpu.VMEM(u_rows.shape, u_rows.dtype),
            pltpu.VMEM(v_cols.shape, v_cols.dtype),
            pltpu.VMEM(weights.shape, weights.dtype),
            pltpu.VMEM((2, 2 * P_SIZE, count), jnp.bfloat16),
            pltpu.VMEM((2, 2 * P_SIZE, count), jnp.bfloat16),
            pltpu.VMEM((2, 2, count // WIDTH, channels * STEP, WIDTH), jnp.float32),
            pltpu.VMEM((2, 2, channels, count), jnp.float32),
            pltpu.VMEM((TERMS, P_SIZE, P_SIZE), jnp.float32),
            pltpu.SemaphoreType.DMA((5,)),
        ],
        compiler_params=pltpu.CompilerParams(vmem_limit_bytes=16 << 20),
    )(*(pltpu.with_memory_space_constraint(x, pltpu.HBM) for x in (crop_start, tau, u_rows, v_cols, weights)))


def whole_patch(parts):
    return pl.pallas_call(
        finish,
        out_shape=jax.ShapeDtypeStruct((TERMS, P_SIZE, P_SIZE), jnp.float32),
        in_specs=[VMEM] * len(parts),
        out_specs=VMEM,
        compiler_params=pltpu.CompilerParams(vmem_limit_bytes=4 << 20),
    )(*parts)


def exchange_orders(chan, space):
    over_chan = [("chan", 1 << b) for b in range(1, chan.bit_length() - 1)]
    over_space = [("space", 1 << b) for b in range(space.bit_length() - 1)]
    orders = []
    for order in (over_chan + over_space, over_space + over_chan):
        swapped = list(order)
        for k in range(0, len(order) - 1, 2):
            swapped[k], swapped[k + 1] = order[k + 1], order[k]
        orders.append(list(zip(order, swapped)))
    return orders


def pairs_of(moves, chan, space):
    pairs = []
    for c in range(chan):
        for s in range(space):
            axis, bit = moves[half_of(c, s)]
            to = (c ^ bit ^ 1, s) if axis == "chan" else (c ^ 1, s ^ bit)
            pairs.append((c * space + s, to[0] * space + to[1]))
    return pairs


def on_device(u_rows, v_cols, weights, tau, crop_start):
    chan, space = lax.axis_size("chan"), lax.axis_size("space")
    partner = [(i, i ^ 1) for i in range(chan)]
    mine_a, other_a, mine_b, other_b = partial_beams(u_rows, v_cols, weights, tau, crop_start)
    totals = [
        mine + lax.ppermute(other, "chan", partner) for mine, other in ((mine_a, other_a), (mine_b, other_b))
    ]
    for phase in zip(*exchange_orders(chan, space)):
        for k, moves in enumerate(phase):
            totals[k] = totals[k] + lax.ppermute(totals[k], ("chan", "space"), pairs_of(moves, chan, space))
    parts = []
    for total in totals:
        parts += [total, lax.ppermute(total, "chan", partner)]
    return whole_patch(parts)


def solution(mesh):
    in_specs = (P("chan", "space"), P("chan", "space"), P("chan", "space"), P("chan"), P())
    return jax.shard_map(on_device, mesh=mesh, in_specs=in_specs, out_specs=P(), check_vma=False)
```

```python
import math

import jax
import jax.numpy as jnp
from jax import lax
from jax.experimental import pallas as pl
from jax.experimental.pallas import tpu as pltpu
from jax.sharding import PartitionSpec as P

G = 8192
P_SIZE = 128
TERMS = 5
STREAMS = 2
ROWS = P_SIZE // STREAMS
HALF = ROWS // 2
STEP = 8
WIDTH = 128
QUARTER = G // 2
MIRROR = P_SIZE // 2


def sin_cos(phase):
    quadrant = (phase + QUARTER // 2) >> (QUARTER.bit_length() - 1)
    rest = phase - quadrant * QUARTER
    x = rest.astype(jnp.float32) * (math.pi / G)
    z = x * x
    s = x + x * z * (-1.6666654611e-1 + z * (8.3321608736e-3 + z * -1.9515295891e-4))
    c = 1.0 - 0.5 * z + z * z * (4.166664568298827e-2 + z * (-1.388731625493765e-3 + z * 2.443315711809948e-5))
    odd = (quadrant & 1) == 1
    sin_value = jnp.where(odd, c, s)
    cos_value = jnp.where(odd, s, c)
    sin_value = jnp.where((quadrant & 2) == 2, -sin_value, sin_value)
    cos_value = jnp.where(((quadrant + 1) & 2) == 2, -cos_value, cos_value)
    return cos_value, sin_value


def double(cos_value, sin_value):
    square = sin_value * sin_value
    return 1.0 - (square + square), (sin_value + sin_value) * cos_value


def prepare(one, first, seeds, steps, group):
    (cos_one, sin_one), (cos_prev, sin_prev) = one, first
    cos_now = cos_prev * cos_one - sin_prev * sin_one
    sin_now = sin_prev * cos_one + cos_prev * sin_one
    twice = cos_one + cos_one
    for row in range(STEP):
        rows = pl.ds(row, cos_one.shape[0], stride=STEP)
        seeds[0, group, rows, :] = cos_prev
        seeds[1, group, rows, :] = sin_prev
        cos_prev, cos_now = cos_now, twice * cos_now - cos_prev
        sin_prev, sin_now = sin_now, twice * sin_now - sin_prev
    chunk = slice(group * WIDTH, (group + 1) * WIDTH)
    steps[0, :, chunk], steps[1, :, chunk] = double(*double(*double(cos_one, sin_one)))


def fill_table(table, chunk, seed, step):
    size = table.shape[0] // 2
    cos_prev, sin_prev = seed
    cos_step, sin_step = (jnp.broadcast_to(value, cos_prev.shape) for value in step)
    cos_now = cos_prev * cos_step - sin_prev * sin_step
    sin_now = sin_prev * cos_step + cos_prev * sin_step
    twice = cos_step + cos_step
    for first in range(0, size, 2 * STEP):
        if first:
            cos_prev = twice * cos_now - cos_prev
            sin_prev = twice * sin_now - sin_prev
            cos_now = twice * cos_prev - cos_now
            sin_now = twice * sin_prev - sin_now
        for base, prev, now in ((first, cos_prev, cos_now), (size + first, sin_prev, sin_now)):
            table[base : base + 2 * STEP, chunk] = jnp.concatenate([prev, now], axis=0).astype(jnp.bfloat16)


def half_of(chan, space):
    bits = chan ^ space
    for shift in (16, 8, 4, 2, 1):
        bits = bits ^ (bits >> shift)
    return bits & 1


def kernel(
    crop_hbm,
    tau_hbm,
    u_hbm,
    v_hbm,
    w_hbm,
    mine_a,
    other_a,
    mine_b,
    other_b,
    crop_ref,
    tau_ref,
    u_ref,
    v_ref,
    w_ref,
    row_tables,
    col_tables,
    seeds,
    steps,
    beams,
    arrived,
):
    channels, count = u_ref.shape
    copies = [
        pltpu.make_async_copy(source, target, arrived.at[k])
        for k, (source, target) in enumerate(
            ((crop_hbm, crop_ref), (u_hbm, u_ref), (v_hbm, v_ref), (w_hbm, w_ref), (tau_hbm, tau_ref))
        )
    ]
    for copy in copies:
        copy.start()
    for copy in copies[:2]:
        copy.wait()
    for group in range(count // WIDTH):
        half_step = sin_cos(u_ref[:, group * WIDTH : (group + 1) * WIDTH])
        prepare(double(*half_step), half_step, seeds.at[0], steps.at[0], group)
    for copy in copies[2:]:
        copy.wait()
    for group in range(count // WIDTH):
        u, v, w = (ref[:, group * WIDTH : (group + 1) * WIDTH] for ref in (u_ref, v_ref, w_ref))
        middle = u * (2 * crop_ref[0] + P_SIZE - 1) + v * (2 * crop_ref[1])
        cos_first, sin_first = sin_cos(middle & (2 * G - 1))
        prepare(sin_cos(v + v), (cos_first * w, sin_first * w), seeds.at[1], steps.at[1], group)

    def fill(channel, slot):
        rows = slice(STEP * channel, STEP * (channel + 1))
        for group in range(0, count // WIDTH, 2):
            chunk = slice(group * WIDTH, (group + 2) * WIDTH)
            for side, tables in enumerate((row_tables, col_tables)):
                seed, step = [], []
                for k in range(2):
                    pair = [seeds[side, k, group + both, rows, :] for both in range(2)]
                    seed.append(jnp.concatenate(pair, axis=1))
                    step.append(steps[side, k, channel : channel + 1, chunk])
                fill_table(tables.at[slot], chunk, seed, step)

    def add(channel, slot):
        product = lax.dot_general(
            row_tables[slot], col_tables[slot], (((1,), (1,)), ((), ())), preferred_element_type=jnp.float32
        )
        even, odd = product[:MIRROR, :P_SIZE], product[MIRROR:, P_SIZE:]
        tau = tau_ref[channel]
        power = None
        for term in range(TERMS):
            for rows, part in ((slice(0, MIRROR), even), (slice(MIRROR, P_SIZE), odd)):
                share = part if power is None else power * part
                beams[term, rows] = share if channel == 0 else beams[term, rows] + share
            power = tau if power is None else power * tau

    fill(0, 0)
    for channel in range(channels):
        if channel + 1 < channels:
            fill(channel + 1, (channel + 1) % 2)
        add(channel, channel % 2)

    squares = jnp.zeros((channels, P_SIZE), jnp.float32)
    for begin in range(0, count, P_SIZE):
        w = w_ref[:, begin : begin + P_SIZE]
        squares += w * w

    mine_a[TERMS * HALF :, :] = squares
    other_a[TERMS * HALF :, :] = squares
    back = STEP - 1 - lax.broadcasted_iota(jnp.int32, (STEP, P_SIZE), 0)

    def block(term, first):
        if first >= MIRROR:
            d = first - MIRROR
            return beams[term, d : d + STEP] - beams[term, MIRROR + d : MIRROR + d + STEP]
        d = MIRROR - STEP - first
        both = beams[term, d : d + STEP] + beams[term, MIRROR + d : MIRROR + d + STEP]
        return jnp.take_along_axis(both, back, axis=0)

    def put(half):
        for k, ref in enumerate((mine_a, other_a, mine_b, other_b)):
            first = first_row(k, half)
            for term in range(TERMS):
                for row in range(0, HALF, STEP):
                    ref[term * HALF + row : term * HALF + row + STEP, :] = block(term, first + row)

    half = half_of(lax.axis_index("chan"), lax.axis_index("space"))
    pl.when(half == 0)(lambda: put(0))
    pl.when(half == 1)(lambda: put(1))


def first_row(k, half):
    return (k // 2) * ROWS + (half ^ (k % 2)) * HALF


def finish(*refs):
    *parts, psf_ref = refs
    squares = parts[0][TERMS * HALF :, :]
    scale = 1.0 / jnp.sqrt(jnp.sum(jnp.sum(squares, axis=1, keepdims=True), axis=0, keepdims=True))

    def put(half):
        for k, ref in enumerate(parts):
            first = first_row(k, half)
            for term in range(TERMS):
                psf_ref[term, first : first + HALF, :] = ref[term * HALF : (term + 1) * HALF, :] * scale

    half = half_of(lax.axis_index("chan"), lax.axis_index("space"))
    pl.when(half == 0)(lambda: put(0))
    pl.when(half == 1)(lambda: put(1))


VMEM = pl.BlockSpec(memory_space=pltpu.VMEM)
HBM = pl.BlockSpec(memory_space=pltpu.HBM)


def partial_beams(u_rows, v_cols, weights, tau, crop_start):
    channels, count = u_rows.shape
    part_a, part_b = (jax.ShapeDtypeStruct((TERMS * HALF + extra, P_SIZE), jnp.float32) for extra in (channels, 0))
    return pl.pallas_call(
        kernel,
        out_shape=(part_a, part_a, part_b, part_b),
        in_specs=[HBM] * 5,
        out_specs=(VMEM,) * 4,
        scratch_shapes=[
            pltpu.SMEM(crop_start.shape, crop_start.dtype),
            pltpu.SMEM(tau.shape, tau.dtype),
            pltpu.VMEM(u_rows.shape, u_rows.dtype),
            pltpu.VMEM(v_cols.shape, v_cols.dtype),
            pltpu.VMEM(weights.shape, weights.dtype),
            pltpu.VMEM((2, 2 * MIRROR, count), jnp.bfloat16),
            pltpu.VMEM((2, 2 * P_SIZE, count), jnp.bfloat16),
            pltpu.VMEM((2, 2, count // WIDTH, STEP * channels, WIDTH), jnp.float32),
            pltpu.VMEM((2, 2, channels, count), jnp.float32),
            pltpu.VMEM((TERMS, P_SIZE, P_SIZE), jnp.float32),
            pltpu.SemaphoreType.DMA((5,)),
        ],
        compiler_params=pltpu.CompilerParams(vmem_limit_bytes=16 << 20),
    )(*(pltpu.with_memory_space_constraint(x, pltpu.HBM) for x in (crop_start, tau, u_rows, v_cols, weights)))


def whole_patch(parts):
    return pl.pallas_call(
        finish,
        out_shape=jax.ShapeDtypeStruct((TERMS, P_SIZE, P_SIZE), jnp.float32),
        in_specs=[VMEM] * len(parts),
        out_specs=VMEM,
        compiler_params=pltpu.CompilerParams(vmem_limit_bytes=4 << 20),
    )(*parts)


def exchange_orders(chan, space):
    over_chan = [("chan", 1 << b) for b in range(1, chan.bit_length() - 1)]
    over_space = [("space", 1 << b) for b in range(space.bit_length() - 1)]
    orders = []
    for order in (over_chan + over_space, over_space + over_chan):
        swapped = list(order)
        for k in range(0, len(order) - 1, 2):
            swapped[k], swapped[k + 1] = order[k + 1], order[k]
        orders.append(list(zip(order, swapped)))
    return orders


def pairs_of(moves, chan, space):
    pairs = []
    for c in range(chan):
        for s in range(space):
            axis, bit = moves[half_of(c, s)]
            to = (c ^ bit ^ 1, s) if axis == "chan" else (c ^ 1, s ^ bit)
            pairs.append((c * space + s, to[0] * space + to[1]))
    return pairs


def on_device(u_rows, v_cols, weights, tau, crop_start):
    chan, space = lax.axis_size("chan"), lax.axis_size("space")
    partner = [(i, i ^ 1) for i in range(chan)]
    mine_a, other_a, mine_b, other_b = partial_beams(u_rows, v_cols, weights, tau, crop_start)
    totals = [
        mine + lax.ppermute(other, "chan", partner) for mine, other in ((mine_a, other_a), (mine_b, other_b))
    ]
    for phase in zip(*exchange_orders(chan, space)):
        for k, moves in enumerate(phase):
            totals[k] = totals[k] + lax.ppermute(totals[k], ("chan", "space"), pairs_of(moves, chan, space))
    parts = []
    for total in totals:
        parts += [total, lax.ppermute(total, "chan", partner)]
    return whole_patch(parts)


def solution(mesh):
    in_specs = (P("chan", "space"), P("chan", "space"), P("chan", "space"), P("chan"), P())
    return jax.shard_map(on_device, mesh=mesh, in_specs=in_specs, out_specs=P(), check_vma=False)
```

```python
import math

import jax
import jax.numpy as jnp
from jax import lax
from jax.experimental import pallas as pl
from jax.experimental.pallas import tpu as pltpu
from jax.sharding import PartitionSpec as P

G = 8192
P_SIZE = 128
TERMS = 5
STREAMS = 2
ROWS = P_SIZE // STREAMS
HALF = ROWS // 2
STEP = 8
WIDTH = 128
QUARTER = G // 2


def sin_cos(phase):
    quadrant = (phase + QUARTER // 2) >> (QUARTER.bit_length() - 1)
    rest = phase - quadrant * QUARTER
    x = rest.astype(jnp.float32) * (math.pi / G)
    z = x * x
    s = x + x * z * (-1.6666654611e-1 + z * (8.3321608736e-3 + z * -1.9515295891e-4))
    c = 1.0 - 0.5 * z + z * z * (4.166664568298827e-2 + z * (-1.388731625493765e-3 + z * 2.443315711809948e-5))
    odd = (quadrant & 1) == 1
    sin_value = jnp.where(odd, c, s)
    cos_value = jnp.where(odd, s, c)
    sin_value = jnp.where((quadrant & 2) == 2, -sin_value, sin_value)
    cos_value = jnp.where(((quadrant + 1) & 2) == 2, -cos_value, cos_value)
    return cos_value, sin_value


def double(cos_value, sin_value):
    square = sin_value * sin_value
    return 1.0 - (square + square), (sin_value + sin_value) * cos_value


def prepare(one, first, seeds, steps, group):
    (cos_one, sin_one), (cos_prev, sin_prev) = one, first
    cos_now = cos_prev * cos_one - sin_prev * sin_one
    sin_now = sin_prev * cos_one + cos_prev * sin_one
    twice = cos_one + cos_one
    for row in range(STEP):
        rows = pl.ds(row, cos_one.shape[0], stride=STEP)
        seeds[0, group, rows, :] = cos_prev
        seeds[1, group, rows, :] = sin_prev
        cos_prev, cos_now = cos_now, twice * cos_now - cos_prev
        sin_prev, sin_now = sin_now, twice * sin_now - sin_prev
    chunk = slice(group * WIDTH, (group + 1) * WIDTH)
    steps[0, :, chunk], steps[1, :, chunk] = double(*double(*double(cos_one, sin_one)))


def fill_table(table, chunk, seed, step):
    size = table.shape[0] // 2
    cos_prev, sin_prev = seed
    cos_step, sin_step = (jnp.broadcast_to(value, cos_prev.shape) for value in step)
    cos_now = cos_prev * cos_step - sin_prev * sin_step
    sin_now = sin_prev * cos_step + cos_prev * sin_step
    twice = cos_step + cos_step
    for first in range(0, size, 2 * STEP):
        if first:
            cos_prev = twice * cos_now - cos_prev
            sin_prev = twice * sin_now - sin_prev
            cos_now = twice * cos_prev - cos_now
            sin_now = twice * sin_prev - sin_now
        for base, prev, now in ((first, cos_prev, cos_now), (size + first, sin_prev, sin_now)):
            table[base : base + 2 * STEP, chunk] = jnp.concatenate([prev, now], axis=0).astype(jnp.bfloat16)


def half_of(chan, space):
    bits = chan ^ space
    for shift in (16, 8, 4, 2, 1):
        bits = bits ^ (bits >> shift)
    return bits & 1


def kernel(
    crop_hbm,
    tau_hbm,
    u_hbm,
    v_hbm,
    w_hbm,
    mine_a,
    other_a,
    mine_b,
    other_b,
    crop_ref,
    tau_ref,
    u_ref,
    v_ref,
    w_ref,
    row_tables,
    col_tables,
    seeds,
    steps,
    beams,
    arrived,
):
    channels, count = u_ref.shape
    copies = [
        pltpu.make_async_copy(source, target, arrived.at[k])
        for k, (source, target) in enumerate(
            ((crop_hbm, crop_ref), (u_hbm, u_ref), (v_hbm, v_ref), (w_hbm, w_ref), (tau_hbm, tau_ref))
        )
    ]
    for copy in copies:
        copy.start()
    for copy in copies[:2]:
        copy.wait()
    for group in range(count // WIDTH):
        u = u_ref[:, group * WIDTH : (group + 1) * WIDTH]
        prepare(sin_cos(u + u), sin_cos((u * (2 * crop_ref[0])) & (2 * G - 1)), seeds.at[0], steps.at[0], group)
    for copy in copies[2:]:
        copy.wait()
    for group in range(count // WIDTH):
        v, w = (ref[:, group * WIDTH : (group + 1) * WIDTH] for ref in (v_ref, w_ref))
        cos_first, sin_first = sin_cos((v * (2 * crop_ref[1])) & (2 * G - 1))
        prepare(sin_cos(v + v), (cos_first * w, sin_first * w), seeds.at[1], steps.at[1], group)

    def fill(channel, slot):
        rows = slice(STEP * channel, STEP * (channel + 1))
        for group in range(0, count // WIDTH, 2):
            chunk = slice(group * WIDTH, (group + 2) * WIDTH)
            for side, tables in enumerate((row_tables, col_tables)):
                seed, step = [], []
                for k in range(2):
                    pair = [seeds[side, k, group + both, rows, :] for both in range(2)]
                    seed.append(jnp.concatenate(pair, axis=1))
                    step.append(steps[side, k, channel : channel + 1, chunk])
                fill_table(tables.at[slot], chunk, seed, step)

    def add(channel, slot):
        product = lax.dot_general(
            row_tables[slot], col_tables[slot], (((1,), (1,)), ((), ())), preferred_element_type=jnp.float32
        )
        beam = product[:P_SIZE, :P_SIZE] - product[P_SIZE:, P_SIZE:]
        tau = tau_ref[channel]
        power = None
        for term in range(TERMS):
            share = beam if power is None else power * beam
            beams[term] = share if channel == 0 else beams[term] + share
            power = tau if power is None else power * tau

    fill(0, 0)
    for channel in range(channels):
        if channel + 1 < channels:
            fill(channel + 1, (channel + 1) % 2)
        add(channel, channel % 2)

    squares = jnp.zeros((channels, P_SIZE), jnp.float32)
    for begin in range(0, count, P_SIZE):
        w = w_ref[:, begin : begin + P_SIZE]
        squares += w * w

    mine_a[TERMS * HALF :, :] = squares
    other_a[TERMS * HALF :, :] = squares

    def put(half):
        for k, ref in enumerate((mine_a, other_a, mine_b, other_b)):
            first = first_row(k, half)
            for term in range(TERMS):
                ref[term * HALF : (term + 1) * HALF, :] = beams[term, first : first + HALF, :]

    half = half_of(lax.axis_index("chan"), lax.axis_index("space"))
    pl.when(half == 0)(lambda: put(0))
    pl.when(half == 1)(lambda: put(1))


def first_row(k, half):
    return (k // 2) * ROWS + (half ^ (k % 2)) * HALF


def finish(*refs):
    *parts, psf_ref = refs
    squares = parts[0][TERMS * HALF :, :]
    scale = 1.0 / jnp.sqrt(jnp.sum(jnp.sum(squares, axis=1, keepdims=True), axis=0, keepdims=True))

    def put(half):
        for k, ref in enumerate(parts):
            first = first_row(k, half)
            for term in range(TERMS):
                psf_ref[term, first : first + HALF, :] = ref[term * HALF : (term + 1) * HALF, :] * scale

    half = half_of(lax.axis_index("chan"), lax.axis_index("space"))
    pl.when(half == 0)(lambda: put(0))
    pl.when(half == 1)(lambda: put(1))


VMEM = pl.BlockSpec(memory_space=pltpu.VMEM)
HBM = pl.BlockSpec(memory_space=pltpu.HBM)


def partial_beams(u_rows, v_cols, weights, tau, crop_start):
    channels, count = u_rows.shape
    part_a, part_b = (jax.ShapeDtypeStruct((TERMS * HALF + extra, P_SIZE), jnp.float32) for extra in (channels, 0))
    return pl.pallas_call(
        kernel,
        out_shape=(part_a, part_a, part_b, part_b),
        in_specs=[HBM] * 5,
        out_specs=(VMEM,) * 4,
        scratch_shapes=[
            pltpu.SMEM(crop_start.shape, crop_start.dtype),
            pltpu.SMEM(tau.shape, tau.dtype),
            pltpu.VMEM(u_rows.shape, u_rows.dtype),
            pltpu.VMEM(v_cols.shape, v_cols.dtype),
            pltpu.VMEM(weights.shape, weights.dtype),
            pltpu.VMEM((2, 2 * P_SIZE, count), jnp.bfloat16),
            pltpu.VMEM((2, 2 * P_SIZE, count), jnp.bfloat16),
            pltpu.VMEM((2, 2, count // WIDTH, STEP * channels, WIDTH), jnp.float32),
            pltpu.VMEM((2, 2, channels, count), jnp.float32),
            pltpu.VMEM((TERMS, P_SIZE, P_SIZE), jnp.float32),
            pltpu.SemaphoreType.DMA((5,)),
        ],
        compiler_params=pltpu.CompilerParams(vmem_limit_bytes=16 << 20),
    )(*(pltpu.with_memory_space_constraint(x, pltpu.HBM) for x in (crop_start, tau, u_rows, v_cols, weights)))


def whole_patch(parts):
    return pl.pallas_call(
        finish,
        out_shape=jax.ShapeDtypeStruct((TERMS, P_SIZE, P_SIZE), jnp.float32),
        in_specs=[VMEM] * len(parts),
        out_specs=VMEM,
        compiler_params=pltpu.CompilerParams(vmem_limit_bytes=4 << 20),
    )(*parts)


def exchange_orders(chan, space):
    over_chan = [("chan", 1 << b) for b in range(1, chan.bit_length() - 1)]
    over_space = [("space", 1 << b) for b in range(space.bit_length() - 1)]
    orders = []
    for order in (over_chan + over_space, over_space + over_chan):
        swapped = list(order)
        for k in range(0, len(order) - 1, 2):
            swapped[k], swapped[k + 1] = order[k + 1], order[k]
        orders.append(list(zip(order, swapped)))
    return orders


def pairs_of(moves, chan, space):
    pairs = []
    for c in range(chan):
        for s in range(space):
            axis, bit = moves[half_of(c, s)]
            to = (c ^ bit ^ 1, s) if axis == "chan" else (c ^ 1, s ^ bit)
            pairs.append((c * space + s, to[0] * space + to[1]))
    return pairs


def on_device(u_rows, v_cols, weights, tau, crop_start):
    chan, space = lax.axis_size("chan"), lax.axis_size("space")
    partner = [(i, i ^ 1) for i in range(chan)]
    mine_a, other_a, mine_b, other_b = partial_beams(u_rows, v_cols, weights, tau, crop_start)
    totals = [
        mine + lax.ppermute(other, "chan", partner) for mine, other in ((mine_a, other_a), (mine_b, other_b))
    ]
    for phase in zip(*exchange_orders(chan, space)):
        for k, moves in enumerate(phase):
            totals[k] = totals[k] + lax.ppermute(totals[k], ("chan", "space"), pairs_of(moves, chan, space))
    parts = []
    for total in totals:
        parts += [total, lax.ppermute(total, "chan", partner)]
    return whole_patch(parts)


def solution(mesh):
    in_specs = (P("chan", "space"), P("chan", "space"), P("chan", "space"), P("chan"), P())
    return jax.shard_map(on_device, mesh=mesh, in_specs=in_specs, out_specs=P(), check_vma=False)
```

```python
import functools
import math

import jax
import jax.numpy as jnp
from jax import lax
from jax.experimental import pallas as pl
from jax.experimental.pallas import tpu as pltpu
from jax.sharding import PartitionSpec as P

G = 8192
P_SIZE = 128
TERMS = 5
STREAMS = 2
ROWS = P_SIZE // STREAMS
HALF = ROWS // 2
STEP = 8
WIDTH = 128
QUARTER = G // 2
MIRROR = P_SIZE // 2


def sin_cos(phase):
    quadrant = (phase + QUARTER // 2) >> (QUARTER.bit_length() - 1)
    rest = phase - quadrant * QUARTER
    x = rest.astype(jnp.float32) * (math.pi / G)
    z = x * x
    s = x + x * z * (-1.6666654611e-1 + z * (8.3321608736e-3 + z * -1.9515295891e-4))
    c = 1.0 - 0.5 * z + z * z * (4.166664568298827e-2 + z * (-1.388731625493765e-3 + z * 2.443315711809948e-5))
    odd = (quadrant & 1) == 1
    sin_value = jnp.where(odd, c, s)
    cos_value = jnp.where(odd, s, c)
    sin_value = jnp.where((quadrant & 2) == 2, -sin_value, sin_value)
    cos_value = jnp.where(((quadrant + 1) & 2) == 2, -cos_value, cos_value)
    return cos_value, sin_value


def double(cos_value, sin_value):
    square = sin_value * sin_value
    return 1.0 - (square + square), (sin_value + sin_value) * cos_value


def prepare(one, first, seeds, steps, group):
    (cos_one, sin_one), (cos_prev, sin_prev) = one, first
    cos_now = cos_prev * cos_one - sin_prev * sin_one
    sin_now = sin_prev * cos_one + cos_prev * sin_one
    twice = cos_one + cos_one
    for row in range(STEP):
        rows = pl.ds(row, cos_one.shape[0], stride=STEP)
        seeds[0, group, rows, :] = cos_prev
        seeds[1, group, rows, :] = sin_prev
        cos_prev, cos_now = cos_now, twice * cos_now - cos_prev
        sin_prev, sin_now = sin_now, twice * sin_now - sin_prev
    chunk = slice(group * WIDTH, (group + 1) * WIDTH)
    steps[0, :, chunk], steps[1, :, chunk] = double(*double(*double(cos_one, sin_one)))


def fill_table(table, chunk, seed, step):
    size = table.shape[0] // 2
    cos_prev, sin_prev = seed
    cos_step, sin_step = (jnp.broadcast_to(value, cos_prev.shape) for value in step)
    cos_now = cos_prev * cos_step - sin_prev * sin_step
    sin_now = sin_prev * cos_step + cos_prev * sin_step
    twice = cos_step + cos_step
    for first in range(0, size, 2 * STEP):
        if first:
            cos_prev = twice * cos_now - cos_prev
            sin_prev = twice * sin_now - sin_prev
            cos_now = twice * cos_prev - cos_now
            sin_now = twice * sin_prev - sin_now
        for base, prev, now in ((first, cos_prev, cos_now), (size + first, sin_prev, sin_now)):
            table[base : base + 2 * STEP, chunk] = jnp.concatenate([prev, now], axis=0).astype(jnp.bfloat16)


def half_of(chan, space):
    bits = chan ^ space
    for shift in (16, 8, 4, 2, 1):
        bits = bits ^ (bits >> shift)
    return bits & 1


def kernel(
    crop_hbm,
    tau_hbm,
    u_hbm,
    v_hbm,
    w_hbm,
    mine_a,
    other_a,
    mine_b,
    other_b,
    crop_ref,
    tau_ref,
    u_ref,
    v_ref,
    w_ref,
    row_tables,
    col_tables,
    seeds,
    steps,
    beams,
    arrived,
):
    channels, count = u_ref.shape
    copies = [
        pltpu.make_async_copy(source, target, arrived.at[k])
        for k, (source, target) in enumerate(
            ((crop_hbm, crop_ref), (u_hbm, u_ref), (v_hbm, v_ref), (w_hbm, w_ref), (tau_hbm, tau_ref))
        )
    ]
    for copy in copies:
        copy.start()
    for copy in copies[:2]:
        copy.wait()
    for group in range(count // WIDTH):
        half_step = sin_cos(u_ref[:, group * WIDTH : (group + 1) * WIDTH])
        prepare(double(*half_step), half_step, seeds.at[0], steps.at[0], group)
    for copy in copies[2:]:
        copy.wait()
    for group in range(count // WIDTH):
        u, v, w = (ref[:, group * WIDTH : (group + 1) * WIDTH] for ref in (u_ref, v_ref, w_ref))
        middle = u * (2 * crop_ref[0] + P_SIZE - 1) + v * (2 * crop_ref[1])
        cos_first, sin_first = sin_cos(middle & (2 * G - 1))
        prepare(sin_cos(v + v), (cos_first * w, sin_first * w), seeds.at[1], steps.at[1], group)

    def fill(channel, slot):
        rows = slice(STEP * channel, STEP * (channel + 1))
        for group in range(0, count // WIDTH, 2):
            chunk = slice(group * WIDTH, (group + 2) * WIDTH)
            for side, tables in enumerate((row_tables, col_tables)):
                seed, step = [], []
                for k in range(2):
                    pair = [seeds[side, k, group + both, rows, :] for both in range(2)]
                    seed.append(jnp.concatenate(pair, axis=1))
                    step.append(steps[side, k, channel : channel + 1, chunk])
                fill_table(tables.at[slot], chunk, seed, step)

    def add(channel, slot):
        product = lax.dot_general(
            row_tables[slot], col_tables[slot], (((1,), (1,)), ((), ())), preferred_element_type=jnp.float32
        )
        even, odd = product[:MIRROR, :P_SIZE], product[MIRROR:, P_SIZE:]
        tau = tau_ref[channel]
        power = None
        for term in range(TERMS):
            for rows, part in ((slice(0, MIRROR), even), (slice(MIRROR, P_SIZE), odd)):
                share = part if power is None else power * part
                beams[term, rows] = share if channel == 0 else beams[term, rows] + share
            power = tau if power is None else power * tau

    fill(0, 0)
    for channel in range(channels):
        if channel + 1 < channels:
            fill(channel + 1, (channel + 1) % 2)
        add(channel, channel % 2)

    squares = jnp.zeros((channels, P_SIZE), jnp.float32)
    for begin in range(0, count, P_SIZE):
        w = w_ref[:, begin : begin + P_SIZE]
        squares += w * w

    mine_a[TERMS * HALF :, :] = squares
    other_a[TERMS * HALF :, :] = squares
    back = STEP - 1 - lax.broadcasted_iota(jnp.int32, (STEP, P_SIZE), 0)

    def block(term, first):
        if first >= MIRROR:
            d = first - MIRROR
            return beams[term, d : d + STEP] - beams[term, MIRROR + d : MIRROR + d + STEP]
        d = MIRROR - STEP - first
        both = beams[term, d : d + STEP] + beams[term, MIRROR + d : MIRROR + d + STEP]
        return jnp.take_along_axis(both, back, axis=0)

    def put(half):
        for k, ref in enumerate((mine_a, other_a, mine_b, other_b)):
            first = first_row(k, half)
            for term in range(TERMS):
                for row in range(0, HALF, STEP):
                    ref[term * HALF + row : term * HALF + row + STEP, :] = block(term, first + row)

    half = half_of(lax.axis_index("chan"), lax.axis_index("space"))
    pl.when(half == 0)(lambda: put(0))
    pl.when(half == 1)(lambda: put(1))


def first_row(k, half):
    return (k // 2) * ROWS + (half ^ (k % 2)) * HALF


def finish(stream, *refs):
    first_ref, mine_ref, away_ref = refs[0], refs[-5], refs[-4]
    psf_hbm, rows_ref, sent = refs[-3:]
    squares = first_ref[TERMS * HALF :, :]
    scale = 1.0 / jnp.sqrt(jnp.sum(jnp.sum(squares, axis=1, keepdims=True), axis=0, keepdims=True))

    def put(half):
        for k, ref in enumerate((mine_ref, away_ref)):
            first = (half ^ k) * HALF
            for term in range(TERMS):
                rows_ref[term, first : first + HALF, :] = ref[term * HALF : (term + 1) * HALF, :] * scale

    half = half_of(lax.axis_index("chan"), lax.axis_index("space"))
    pl.when(half == 0)(lambda: put(0))
    pl.when(half == 1)(lambda: put(1))
    copy = pltpu.make_async_copy(rows_ref, psf_hbm.at[:, stream * ROWS : (stream + 1) * ROWS, :], sent)
    copy.start()
    copy.wait()


VMEM = pl.BlockSpec(memory_space=pltpu.VMEM)
HBM = pl.BlockSpec(memory_space=pltpu.HBM)


def partial_beams(u_rows, v_cols, weights, tau, crop_start):
    channels, count = u_rows.shape
    part_a, part_b = (jax.ShapeDtypeStruct((TERMS * HALF + extra, P_SIZE), jnp.float32) for extra in (channels, 0))
    return pl.pallas_call(
        kernel,
        out_shape=(part_a, part_a, part_b, part_b),
        in_specs=[HBM] * 5,
        out_specs=(VMEM,) * 4,
        scratch_shapes=[
            pltpu.SMEM(crop_start.shape, crop_start.dtype),
            pltpu.SMEM(tau.shape, tau.dtype),
            pltpu.VMEM(u_rows.shape, u_rows.dtype),
            pltpu.VMEM(v_cols.shape, v_cols.dtype),
            pltpu.VMEM(weights.shape, weights.dtype),
            pltpu.VMEM((2, 2 * MIRROR, count), jnp.bfloat16),
            pltpu.VMEM((2, 2 * P_SIZE, count), jnp.bfloat16),
            pltpu.VMEM((2, 2, count // WIDTH, STEP * channels, WIDTH), jnp.float32),
            pltpu.VMEM((2, 2, channels, count), jnp.float32),
            pltpu.VMEM((TERMS, P_SIZE, P_SIZE), jnp.float32),
            pltpu.SemaphoreType.DMA((5,)),
        ],
        compiler_params=pltpu.CompilerParams(vmem_limit_bytes=16 << 20),
    )(*(pltpu.with_memory_space_constraint(x, pltpu.HBM) for x in (crop_start, tau, u_rows, v_cols, weights)))


def whole_patch(parts):
    psf = None
    for stream in range(STREAMS):
        args = [parts[0]] + ([] if psf is None else [psf]) + parts[2 * stream : 2 * stream + 2]
        psf = pl.pallas_call(
            functools.partial(finish, stream),
            out_shape=jax.ShapeDtypeStruct((TERMS, P_SIZE, P_SIZE), jnp.float32),
            in_specs=[VMEM] + ([] if psf is None else [HBM]) + [VMEM, VMEM],
            out_specs=HBM,
            input_output_aliases={} if psf is None else {1: 0},
            scratch_shapes=[pltpu.VMEM((TERMS, ROWS, P_SIZE), jnp.float32), pltpu.SemaphoreType.DMA],
            compiler_params=pltpu.CompilerParams(vmem_limit_bytes=4 << 20),
        )(*args)
    return psf


def exchange_orders(chan, space):
    over_chan = [("chan", 1 << b) for b in range(1, chan.bit_length() - 1)]
    over_space = [("space", 1 << b) for b in range(space.bit_length() - 1)]
    orders = []
    for order in (over_chan + over_space, over_space + over_chan):
        swapped = list(order)
        for k in range(0, len(order) - 1, 2):
            swapped[k], swapped[k + 1] = order[k + 1], order[k]
        orders.append(list(zip(order, swapped)))
    return orders


def pairs_of(moves, chan, space):
    pairs = []
    for c in range(chan):
        for s in range(space):
            axis, bit = moves[half_of(c, s)]
            to = (c ^ bit ^ 1, s) if axis == "chan" else (c ^ 1, s ^ bit)
            pairs.append((c * space + s, to[0] * space + to[1]))
    return pairs


def on_device(u_rows, v_cols, weights, tau, crop_start):
    chan, space = lax.axis_size("chan"), lax.axis_size("space")
    partner = [(i, i ^ 1) for i in range(chan)]
    mine_a, other_a, mine_b, other_b = partial_beams(u_rows, v_cols, weights, tau, crop_start)
    totals = [
        mine + lax.ppermute(other, "chan", partner) for mine, other in ((mine_a, other_a), (mine_b, other_b))
    ]
    for phase in zip(*exchange_orders(chan, space)):
        for k, moves in enumerate(phase):
            totals[k] = totals[k] + lax.ppermute(totals[k], ("chan", "space"), pairs_of(moves, chan, space))
    parts = []
    for total in totals:
        parts += [total, lax.ppermute(total, "chan", partner)]
    return whole_patch(parts)


def solution(mesh):
    in_specs = (P("chan", "space"), P("chan", "space"), P("chan", "space"), P("chan"), P())
    return jax.shard_map(on_device, mesh=mesh, in_specs=in_specs, out_specs=P(), check_vma=False)
```

```python
import functools
import math

import jax
import jax.numpy as jnp
from jax import lax
from jax.experimental import pallas as pl
from jax.experimental.pallas import tpu as pltpu
from jax.sharding import PartitionSpec as P

G = 8192
P_SIZE = 128
TERMS = 5
STREAMS = 2
ROWS = P_SIZE // STREAMS
HALF = ROWS // 2
STEP = 8
WIDTH = 128
QUARTER = G // 2
MIRROR = P_SIZE // 2


def sin_cos(phase):
    quadrant = (phase + QUARTER // 2) >> (QUARTER.bit_length() - 1)
    rest = phase - quadrant * QUARTER
    x = rest.astype(jnp.float32) * (math.pi / G)
    z = x * x
    s = x + x * z * (-1.6666654611e-1 + z * (8.3321608736e-3 + z * -1.9515295891e-4))
    c = 1.0 - 0.5 * z + z * z * (4.166664568298827e-2 + z * (-1.388731625493765e-3 + z * 2.443315711809948e-5))
    odd = (quadrant & 1) == 1
    sin_value = jnp.where(odd, c, s)
    cos_value = jnp.where(odd, s, c)
    sin_value = jnp.where((quadrant & 2) == 2, -sin_value, sin_value)
    cos_value = jnp.where(((quadrant + 1) & 2) == 2, -cos_value, cos_value)
    return cos_value, sin_value


def double(cos_value, sin_value):
    square = sin_value * sin_value
    return 1.0 - (square + square), (sin_value + sin_value) * cos_value


def prepare(one, first, seeds, steps, group):
    (cos_one, sin_one), (cos_prev, sin_prev) = one, first
    cos_now = cos_prev * cos_one - sin_prev * sin_one
    sin_now = sin_prev * cos_one + cos_prev * sin_one
    twice = cos_one + cos_one
    for row in range(STEP):
        rows = pl.ds(row, cos_one.shape[0], stride=STEP)
        seeds[0, group, rows, :] = cos_prev
        seeds[1, group, rows, :] = sin_prev
        cos_prev, cos_now = cos_now, twice * cos_now - cos_prev
        sin_prev, sin_now = sin_now, twice * sin_now - sin_prev
    chunk = slice(group * WIDTH, (group + 1) * WIDTH)
    steps[0, :, chunk], steps[1, :, chunk] = double(*double(*double(cos_one, sin_one)))


def fill_table(table, chunk, seed, step):
    size = table.shape[0] // 2
    cos_prev, sin_prev = seed
    cos_step, sin_step = (jnp.broadcast_to(value, cos_prev.shape) for value in step)
    cos_now = cos_prev * cos_step - sin_prev * sin_step
    sin_now = sin_prev * cos_step + cos_prev * sin_step
    twice = cos_step + cos_step
    for first in range(0, size, 2 * STEP):
        if first:
            cos_prev = twice * cos_now - cos_prev
            sin_prev = twice * sin_now - sin_prev
            cos_now = twice * cos_prev - cos_now
            sin_now = twice * sin_prev - sin_now
        for base, prev, now in ((first, cos_prev, cos_now), (size + first, sin_prev, sin_now)):
            table[base : base + 2 * STEP, chunk] = jnp.concatenate([prev, now], axis=0).astype(jnp.bfloat16)


def half_of(chan, space):
    bits = chan ^ space
    for shift in (16, 8, 4, 2, 1):
        bits = bits ^ (bits >> shift)
    return bits & 1


def kernel(
    crop_hbm,
    tau_hbm,
    u_hbm,
    v_hbm,
    w_hbm,
    mine_a,
    other_a,
    mine_b,
    other_b,
    crop_ref,
    tau_ref,
    u_ref,
    v_ref,
    w_ref,
    row_tables,
    col_tables,
    seeds,
    steps,
    beams,
    arrived,
):
    channels, count = u_ref.shape
    copies = [
        pltpu.make_async_copy(source, target, arrived.at[k])
        for k, (source, target) in enumerate(
            ((crop_hbm, crop_ref), (u_hbm, u_ref), (v_hbm, v_ref), (w_hbm, w_ref), (tau_hbm, tau_ref))
        )
    ]
    for copy in copies:
        copy.start()
    for copy in copies[:2]:
        copy.wait()
    for group in range(count // WIDTH):
        half_step = sin_cos(u_ref[:, group * WIDTH : (group + 1) * WIDTH])
        prepare(double(*half_step), half_step, seeds.at[0], steps.at[0], group)
    for copy in copies[2:]:
        copy.wait()
    for group in range(count // WIDTH):
        u, v, w = (ref[:, group * WIDTH : (group + 1) * WIDTH] for ref in (u_ref, v_ref, w_ref))
        middle = u * (2 * crop_ref[0] + P_SIZE - 1) + v * (2 * crop_ref[1])
        cos_first, sin_first = sin_cos(middle & (2 * G - 1))
        prepare(sin_cos(v + v), (cos_first * w, sin_first * w), seeds.at[1], steps.at[1], group)

    def fill(channel, slot):
        rows = slice(STEP * channel, STEP * (channel + 1))
        for group in range(0, count // WIDTH, 2):
            chunk = slice(group * WIDTH, (group + 2) * WIDTH)
            for side, tables in enumerate((row_tables, col_tables)):
                seed, step = [], []
                for k in range(2):
                    pair = [seeds[side, k, group + both, rows, :] for both in range(2)]
                    seed.append(jnp.concatenate(pair, axis=1))
                    step.append(steps[side, k, channel : channel + 1, chunk])
                fill_table(tables.at[slot], chunk, seed, step)

    def add(channel, slot):
        product = lax.dot_general(
            row_tables[slot], col_tables[slot], (((1,), (1,)), ((), ())), preferred_element_type=jnp.float32
        )
        even, odd = product[:MIRROR, :P_SIZE], product[MIRROR:, P_SIZE:]
        tau = tau_ref[channel]
        power = None
        for term in range(TERMS):
            for rows, part in ((slice(0, MIRROR), even), (slice(MIRROR, P_SIZE), odd)):
                share = part if power is None else power * part
                beams[term, rows] = share if channel == 0 else beams[term, rows] + share
            power = tau if power is None else power * tau

    fill(0, 0)
    for channel in range(channels):
        if channel + 1 < channels:
            fill(channel + 1, (channel + 1) % 2)
        add(channel, channel % 2)

    squares = jnp.zeros((channels, P_SIZE), jnp.float32)
    for begin in range(0, count, P_SIZE):
        w = w_ref[:, begin : begin + P_SIZE]
        squares += w * w

    mine_a[TERMS * HALF :, :] = squares
    other_a[TERMS * HALF :, :] = squares
    back = STEP - 1 - lax.broadcasted_iota(jnp.int32, (STEP, P_SIZE), 0)

    def block(term, first):
        if first >= MIRROR:
            d = first - MIRROR
            return beams[term, d : d + STEP] - beams[term, MIRROR + d : MIRROR + d + STEP]
        d = MIRROR - STEP - first
        both = beams[term, d : d + STEP] + beams[term, MIRROR + d : MIRROR + d + STEP]
        return jnp.take_along_axis(both, back, axis=0)

    def put(half):
        for k, ref in enumerate((mine_a, other_a, mine_b, other_b)):
            first = first_row(k, half)
            for term in range(TERMS):
                for row in range(0, HALF, STEP):
                    ref[term * HALF + row : term * HALF + row + STEP, :] = block(term, first + row)

    half = half_of(lax.axis_index("chan"), lax.axis_index("space"))
    pl.when(half == 0)(lambda: put(0))
    pl.when(half == 1)(lambda: put(1))


def first_row(k, half):
    return (k // 2) * ROWS + (half ^ (k % 2)) * HALF


def finish(stream, *refs):
    first_ref, mine_ref, away_ref = refs[0], refs[-5], refs[-4]
    psf_hbm, rows_ref, sent = refs[-3:]
    squares = first_ref[TERMS * HALF :, :]
    scale = 1.0 / jnp.sqrt(jnp.sum(jnp.sum(squares, axis=1, keepdims=True), axis=0, keepdims=True))

    def put(half):
        for k, ref in enumerate((mine_ref, away_ref)):
            first = (half ^ k) * HALF
            for term in range(TERMS):
                rows_ref[term, first : first + HALF, :] = ref[term * HALF : (term + 1) * HALF, :] * scale

    half = half_of(lax.axis_index("chan"), lax.axis_index("space"))
    pl.when(half == 0)(lambda: put(0))
    pl.when(half == 1)(lambda: put(1))
    copy = pltpu.make_async_copy(rows_ref, psf_hbm.at[:, stream * ROWS : (stream + 1) * ROWS, :], sent)
    copy.start()
    copy.wait()


VMEM = pl.BlockSpec(memory_space=pltpu.VMEM)
HBM = pl.BlockSpec(memory_space=pltpu.HBM)


def partial_beams(u_rows, v_cols, weights, tau, crop_start):
    channels, count = u_rows.shape
    part_a, part_b = (jax.ShapeDtypeStruct((TERMS * HALF + extra, P_SIZE), jnp.float32) for extra in (channels, 0))
    return pl.pallas_call(
        kernel,
        out_shape=(part_a, part_a, part_b, part_b),
        in_specs=[HBM] * 5,
        out_specs=(VMEM,) * 4,
        scratch_shapes=[
            pltpu.SMEM(crop_start.shape, crop_start.dtype),
            pltpu.SMEM(tau.shape, tau.dtype),
            pltpu.VMEM(u_rows.shape, u_rows.dtype),
            pltpu.VMEM(v_cols.shape, v_cols.dtype),
            pltpu.VMEM(weights.shape, weights.dtype),
            pltpu.VMEM((2, 2 * MIRROR, count), jnp.bfloat16),
            pltpu.VMEM((2, 2 * P_SIZE, count), jnp.bfloat16),
            pltpu.VMEM((2, 2, count // WIDTH, STEP * channels, WIDTH), jnp.float32),
            pltpu.VMEM((2, 2, channels, count), jnp.float32),
            pltpu.VMEM((TERMS, P_SIZE, P_SIZE), jnp.float32),
            pltpu.SemaphoreType.DMA((5,)),
        ],
        compiler_params=pltpu.CompilerParams(vmem_limit_bytes=16 << 20),
    )(*(pltpu.with_memory_space_constraint(x, pltpu.HBM) for x in (crop_start, tau, u_rows, v_cols, weights)))


def whole_patch(parts):
    psf = None
    for stream in range(STREAMS):
        args = [parts[0]] + ([] if psf is None else [psf]) + parts[2 * stream : 2 * stream + 2]
        psf = pl.pallas_call(
            functools.partial(finish, stream),
            out_shape=jax.ShapeDtypeStruct((TERMS, P_SIZE, P_SIZE), jnp.float32),
            in_specs=[VMEM] + ([] if psf is None else [HBM]) + [VMEM, VMEM],
            out_specs=HBM,
            input_output_aliases={} if psf is None else {1: 0},
            scratch_shapes=[pltpu.VMEM((TERMS, ROWS, P_SIZE), jnp.float32), pltpu.SemaphoreType.DMA],
            compiler_params=pltpu.CompilerParams(vmem_limit_bytes=4 << 20),
        )(*args)
    return psf


def exchange_orders(chan, space):
    over_chan = [("chan", 1 << b) for b in range(1, chan.bit_length() - 1)]
    over_space = [("space", 1 << b) for b in range(space.bit_length() - 1)]
    middle = len(over_space) // 2
    order = over_space[:middle] + over_chan + over_space[middle:]
    swapped = list(order)
    for k in range(0, len(order) - 1, 2):
        swapped[k], swapped[k + 1] = order[k + 1], order[k]
    return [list(zip(order, swapped)), list(zip(swapped[::-1], order[::-1]))]


def pairs_of(moves, chan, space):
    pairs = []
    for c in range(chan):
        for s in range(space):
            axis, bit = moves[half_of(c, s)]
            to = (c ^ bit ^ 1, s) if axis == "chan" else (c ^ 1, s ^ bit)
            pairs.append((c * space + s, to[0] * space + to[1]))
    return pairs


def on_device(u_rows, v_cols, weights, tau, crop_start):
    chan, space = lax.axis_size("chan"), lax.axis_size("space")
    partner = [(i, i ^ 1) for i in range(chan)]
    mine_a, other_a, mine_b, other_b = partial_beams(u_rows, v_cols, weights, tau, crop_start)
    totals = [
        mine + lax.ppermute(other, "chan", partner) for mine, other in ((mine_a, other_a), (mine_b, other_b))
    ]
    for phase in zip(*exchange_orders(chan, space)):
        for k, moves in enumerate(phase):
            totals[k] = totals[k] + lax.ppermute(totals[k], ("chan", "space"), pairs_of(moves, chan, space))
    parts = []
    for total in totals:
        parts += [total, lax.ppermute(total, "chan", partner)]
    return whole_patch(parts)


def solution(mesh):
    in_specs = (P("chan", "space"), P("chan", "space"), P("chan", "space"), P("chan"), P())
    return jax.shard_map(on_device, mesh=mesh, in_specs=in_specs, out_specs=P(), check_vma=False)
```
